512 devices in a mesh: row: 16 (over z, core), col: 32 (over y, x).
Axes of the slice: x: 4, y: 8, z: 8, core: 2. Of those that a mesh axis runs over, the one named last changes fastest.
Arguments:
- tokens: bfloat16 [2048, 8192], P('col', 'row'), may hold values from -6 to 6
- gate_weight: bfloat16 [8192, 16384], P('row', 'col'), may hold values from -0.0625 to 0.0625
- up_weight: bfloat16 [8192, 16384], P('row', 'col'), may hold values from -0.0625 to 0.0625
- block_mask: int32 [64, 128], P('row', 'col'), may hold values 0 or 1
- hidden_grad: bfloat16 [2048, 16384], P('row', 'col'), may hold values from -0.13183594 to 0.13183594
Outputs:
- hidden: bfloat16 [2048, 16384], P('row', 'col')
- gate_weight_grad: float32 [8192, 16384], P('row', 'col')
- up_weight_grad: float32 [8192, 16384], P('row', 'col')
The draws below stay inside these ranges and needn't reach their ends.
All inputs are finite; a program needn't handle non-finite values. No bound on the sum of `block_mask` on one device may be relied on, other than what follows from the above.
Results may differ from the reference program's by a relative error of at most 0.003.
Values may be sent and summed in bfloat16 or wider, within the bound.
A program may use at most 64 MiB of HBM per device.

```python
import jax
import jax.numpy as jnp

D = 8192
FF = 16384
BLOCK = 128
TOKENS = 2048


def with_ends(result, stream_key, low, top_value):
    longest = result.shape.index(max(result.shape))
    spots = []
    for shift in (0, 1):
        where = [jax.random.randint(jax.random.fold_in(stream_key, axis), (), 0, length) for axis, length in enumerate(result.shape)]
        where[longest] = (where[longest] + shift) % result.shape[longest]
        spots.append(tuple(where))
    return result.at[spots[0]].set(low).at[spots[1]].set(top_value)


def block_scale(key, extent, split, low, high):
    factor_of = 1.0
    for position, blocks in split:
        draws = jax.random.uniform(jax.random.fold_in(jax.random.fold_in(key, 6), position), (blocks,), jnp.float32, low / len(split), high / len(split))
        factor_of = factor_of * jnp.repeat(jnp.exp(draws), extent[position] // blocks).reshape((-1,) + (1,) * (len(extent) - 1 - position))
    return factor_of


def normal_values(own_key, extent, scale, limit, cuts=(), dtype=jnp.bfloat16):
    loudness = block_scale(own_key, extent, cuts, -0.22, 0.18) if cuts else 1.0
    values = jax.random.normal(own_key, extent, jnp.float32) * scale * loudness
    return jnp.minimum(jnp.maximum(values, -limit), limit).astype(dtype)


def setup_inputs(seed: int = 0) -> dict:
    key_of = jax.random.split(jax.random.key(seed), 6)
    tokens = normal_values(key_of[0], (TOKENS, D), 1.0, 6.0, ((0, 32), (1, 16)))
    gate_weight = normal_values(key_of[1], (D, FF), D ** -0.5, 0.0625, ((0, 16), (1, 32)))
    up_weight = normal_values(key_of[2], (D, FF), D ** -0.5, 0.0625, ((0, 16), (1, 32)))
    block_mask = with_ends((jax.random.randint(key_of[3], (D // BLOCK, FF // BLOCK), 0, 2) < 1).astype(jnp.int32), jax.random.fold_in(key_of[3], 1), 0, 1)
    hidden_grad = normal_values(key_of[4], (TOKENS, FF), (TOKENS ** -0.5), 0.13183594, ((0, 16), (1, 32)))
    return dict(tokens=tokens, gate_weight=gate_weight, up_weight=up_weight, block_mask=block_mask, hidden_grad=hidden_grad)


def spread(block_mask):
    rows, cols = block_mask.shape
    ones = block_mask.astype(jnp.bfloat16)
    wide = jnp.broadcast_to(ones[:, None, :, None], (rows, BLOCK, cols, BLOCK))
    return wide.reshape(rows * BLOCK, cols * BLOCK)


def local_grads(gate, up, cotangent):
    sig = jax.nn.sigmoid(gate)
    silu = gate * sig
    hidden = (silu * up).astype(jnp.bfloat16)
    back = cotangent.astype(jnp.float32)
    gate_delta = (back * up * sig * (1.0 + gate * (1.0 - sig))).astype(jnp.bfloat16)
    up_delta = (back * silu).astype(jnp.bfloat16)
    return hidden, gate_delta, up_delta


def reference(tokens, gate_weight, up_weight, block_mask, hidden_grad):
    keep = spread(block_mask)
    stacked = jnp.concatenate([gate_weight * keep, up_weight * keep], axis=1)
    both = jnp.dot(tokens, stacked, preferred_element_type=jnp.float32)
    hidden, gate_delta, up_delta = local_grads(both[:, :FF], both[:, FF:], hidden_grad)
    deltas = jnp.concatenate([gate_delta, up_delta], axis=1)
    grads = jnp.dot(tokens.T, deltas, preferred_element_type=jnp.float32)
    keep_wide = keep.astype(jnp.float32)
    return hidden, grads[:, :FF] * keep_wide, grads[:, FF:] * keep_wide
```

```python
import jax
import jax.numpy as jnp
from jax import lax
from jax.experimental import pallas as pl
from jax.experimental.pallas import tpu as pltpu
from jax.sharding import PartitionSpec as P

MESH = pl.DeviceIdType.MESH
BF16, F32 = jnp.bfloat16, jnp.float32
X, Y, Z = 4, 8, 8
BLOCK = 128
TOK = 64
HALF = 32
FEAT = 512
CHUNKS = 4
WIDE = 2 * BLOCK
SCALE = 2.0**17

FIRST = {1: (0, 2), -1: (1, 3)}
NEXT = {1: (1, 0, 3, 2), -1: (0, 1, 2, 3)}
SUMS = {s: [(4, k) for k in FIRST[s]] + [(d, k) for d in (3, 2, 1) for k in NEXT[s]] for s in (1, -1)}
LAST = {1: (0, 1), -1: (2, 3)}


class Links:
    def __init__(self, send_sems, recv_sems):
        self.send_sems, self.recv_sems = send_sems, recv_sems
        self.ids, self.sent = {}, []

    def number(self, key):
        return self.ids.setdefault(key, len(self.ids))

    def copy(self, key, src, dst, device):
        n = self.number(key)
        return pltpu.make_async_remote_copy(
            src_ref=src,
            dst_ref=dst,
            send_sem=self.send_sems.at[n],
            recv_sem=self.recv_sems.at[n],
            device_id=device,
            device_id_type=MESH,
        )

    def send(self, key, src, dst, device):
        copy = self.copy(key, src, dst, device)
        copy.start()
        self.sent.append(copy)

    def recv(self, key, dst, device):
        self.copy(key, dst, dst, device).wait_recv()

    def finish(self):
        for copy in self.sent:
            copy.wait_send()


def encode(v):
    return (v * jnp.abs(v) * (v * v)).astype(BF16)


def decode(code):
    y = code.astype(F32)
    root = lax.rsqrt(lax.rsqrt(jnp.abs(y)))
    return jnp.where(y < 0.0, -root, root)


def kernel(
    tok, gate_w, up_w, mask, cot, hidden, gate_grad, up_grad,
    tall, tsib, flip, own_w, sib_w, delta, acc, sums_out, sums_in, send_sems, recv_sems,
):
    row, col = lax.axis_index("row"), lax.axis_index("col")
    z, core = lax.div(row, 2), lax.rem(row, 2)
    y, x = lax.div(col, X), lax.rem(col, X)
    links = Links(send_sems, recv_sems)
    xs = lambda d: lax.rem(x + d + X, X)
    ys = lambda d: lax.rem(y + d + Y, Y)
    zs = lambda d: lax.rem(z + d + Z, Z)
    sibling = (z * 2 + 1 - core, col)
    xdev = {s: (row, y * X + xs(s)) for s in (1, -1)}
    ydev = {s: (row, ys(s) * X + x) for s in (1, -1)}
    zdev = {s: (zs(s) * 2 + core, col) for s in (1, -1)}

    for i in range(FEAT // BLOCK):
        rows = slice(i * BLOCK, (i + 1) * BLOCK)
        for k in range(CHUNKS):
            cols = slice(k * BLOCK, (k + 1) * BLOCK)
            keep = mask[i, k].astype(F32) * SCALE
            own_w[k, rows, :BLOCK] = (gate_w[rows, cols].astype(F32) * keep).astype(BF16)
            own_w[k, rows, BLOCK:] = (up_w[rows, cols].astype(F32) * keep).astype(BF16)

    barrier = pltpu.get_barrier_semaphore()
    partners = [sibling, *xdev.values(), *ydev.values(), *zdev.values()]
    for device in partners:
        pl.semaphore_signal(barrier, inc=1, device_id=device, device_id_type=MESH)
    pl.semaphore_wait(barrier, len(partners))

    a, b = pl.ds(0, HALF), pl.ds(HALF, TOK - HALF)
    q = HALF // 2
    quarter = {("a", 1): pl.ds(0, q), ("a", -1): pl.ds(q, q), ("b", 1): pl.ds(HALF, q), ("b", -1): pl.ds(HALF + q, q)}
    for s in (1, -1):
        links.send(("xa", s), tok.at[a], tall.at[y, x, a], xdev[s])
        links.send(("yb", s, 1), tok.at[b], tall.at[y, x, b], ydev[s])
    for s in (1, -1):
        links.send(("ya", s, 1, 0), tok.at[a], tall.at[y, x, a], ydev[s])
        links.send(("xb", s, 0), tok.at[b], tall.at[y, x, b], xdev[s])
    for k in range(CHUNKS):
        links.send(("w", k), own_w.at[k], sib_w.at[k], sibling)
    tall[y, x] = tok[...]

    def ya_send(s, d, dx, part):
        ref = tall.at[ys(-(d - 1) * s), xs(dx), part]
        links.send(("ya", s, d, dx), ref, ref, ydev[s])

    def ya_recv(s, d, dx):
        part = a if d < 4 else quarter["a", s]
        links.recv(("ya", s, d, dx), tall.at[ys(-d * s), xs(dx), part], ydev[s])

    def ya_step(d):
        for dx in (0, -1, 1, 2):
            for s in (1, -1):
                ya_recv(s, d, dx)
                if d < 4:
                    ya_send(s, d + 1, dx, a if d < 3 else quarter["a", s])

    def yb_step(d):
        for s in (1, -1):
            part = b if d < 4 else quarter["b", s]
            ref = tall.at[ys(-d * s), x, part]
            links.recv(("yb", s, d), ref, ydev[s])
            if d < 4:
                ref = tall.at[ys(-d * s), x, b if d < 3 else quarter["b", s]]
                links.send(("yb", s, d + 1), ref, ref, ydev[s])
        for dy in (-d, d) if d < 4 else (4,):
            ref = tall.at[ys(dy), x, b]
            for s in (1, -1):
                links.send(("xb", s, dy), ref, ref, xdev[s])

    def xb_step(dy):
        for s in (1, -1):
            links.recv(("xb", s, dy), tall.at[ys(dy), xs(-s), b], xdev[s])
            ref = tall.at[ys(dy), xs(-s), quarter["b", s]]
            links.send(("xb2", s, dy), ref, ref, xdev[s])

    for s in (1, -1):
        links.recv(("xa", s), tall.at[y, xs(-s), a], xdev[s])
        ref = tall.at[y, xs(-s), quarter["a", s]]
        links.send(("xa2", s), ref, ref, xdev[s])
        for t in (1, -1):
            ya_send(t, 1, -s, a)
    yb_step(1)
    for s in (1, -1):
        links.recv(("xa2", s), tall.at[y, xs(2), quarter["a", s]], xdev[s])
    for t in (1, -1):
        ya_send(t, 1, 2, a)
    xb_step(0)
    yb_step(2)
    xb_step(-1)
    xb_step(1)
    ya_step(1)
    yb_step(3)
    xb_step(-2)
    xb_step(2)
    yb_step(4)
    ya_step(2)
    xb_step(-3)
    xb_step(3)
    ya_step(3)
    xb_step(4)

    other = pl.ds(2 * (1 - core), 2)
    for dy in (0, -1, 1, -2, 2, -3, 3, 4):
        if dy == 4:
            ya_step(4)
        for s in (1, -1):
            links.recv(("xb2", s, dy), tall.at[ys(dy), xs(2), quarter["b", s]], xdev[s])
        links.send(("t", dy), tall.at[ys(dy), other], tsib.at[ys(dy)], sibling)
    for k in range(CHUNKS):
        links.recv(("w", k), sib_w.at[k], sibling)
    for dy in (0, -1, 1, -2, 2, -3, 3, 4):
        links.recv(("t", dy), tsib.at[ys(dy)], sibling)

    mine = pl.ds(2 * core, 2)

    def partial(level, k):
        own = tall[level, mine].reshape(BLOCK, FEAT)
        sib = tsib[level].reshape(BLOCK, FEAT)
        return jnp.dot(own, own_w[k], preferred_element_type=F32) + jnp.dot(sib, sib_w[k], preferred_element_type=F32)

    def flip_level(level):
        flip[level, :, :BLOCK] = jnp.transpose(tall[level, mine].reshape(BLOCK, FEAT))
        flip[level, :, BLOCK:] = jnp.transpose(tall[level, other].reshape(BLOCK, FEAT))

    side = {1: 0, -1: 1}
    slots = {s: {dk: i for i, dk in enumerate(SUMS[s])} for s in (1, -1)}

    def arrived(s, d, k):
        i = slots[s][d, k]
        links.recv(("sum", s, i), sums_in.at[side[s], i], zdev[s])
        return decode(sums_in[side[s], i])

    for i in range(len(SUMS[1])):
        for s in (1, -1):
            d, k = SUMS[s][i]
            total = partial(zs(d * s), k)
            if d < 4 and (d + 1, k) in slots[s]:
                total += arrived(s, d + 1, k)
            sums_out[side[s], i] = encode(total)
            links.send(("sum", s, i), sums_out.at[side[s], i], sums_in.at[side[s], i], zdev[s])
        if i < Z:
            flip_level(i)

    for k in range(CHUNKS):
        both = (partial(z, k) + arrived(1, 1, k) + arrived(-1, 1, k)) * (1.0 / SCALE)
        cols = slice(k * BLOCK, (k + 1) * BLOCK)
        gate, up = both[:, :BLOCK], both[:, BLOCK:]
        sig = 1.0 / (1.0 + jnp.exp(-gate))
        silu = gate * sig
        back = cot[:, cols].astype(F32)
        hidden[:, cols] = (silu * up).astype(BF16)
        delta[z, k, :BLOCK, :BLOCK] = (back * up * sig * (1.0 + gate * (1.0 - sig))).astype(BF16)
        delta[z, k, :BLOCK, BLOCK:] = (back * silu).astype(BF16)
        ref = delta.at[z, k, pl.ds(0, BLOCK)]
        for s in (1, -1):
            links.send(("delta", s, 1, k), ref, ref, zdev[s])
        links.send(("pass", 0, k), ref, delta.at[z, k, pl.ds(BLOCK, BLOCK)], sibling)

    def add(level, k, name, first=False):
        links.recv(name, delta.at[level, k, pl.ds(BLOCK, BLOCK)], sibling)
        term = jnp.dot(flip[level], delta[level, k], preferred_element_type=F32)
        if first:
            acc[k] = term
        else:
            acc[k] += term

    waiting = [(z, k, ("pass", 0, k), True) for k in range(CHUNKS)]
    for d in (1, 2, 3, 4):
        for k in range(CHUNKS):
            later = []
            for s in (1, -1):
                if d == 4 and k not in LAST[s]:
                    continue
                level = zs(-d * s)
                ref = delta.at[level, k, pl.ds(0, BLOCK)]
                links.recv(("delta", s, d, k), ref, zdev[s])
                if d < 3 or (d == 3 and k in LAST[s]):
                    links.send(("delta", s, d + 1, k), ref, ref, zdev[s])
                links.send(("pass", d * s, k), ref, delta.at[level, k, pl.ds(BLOCK, BLOCK)], sibling)
                later.append((level, k, ("pass", d * s, k), False))
            while len(waiting) > (3 if d < 4 else 0):
                add(*waiting.pop(0))
            waiting += later
    while waiting:
        add(*waiting.pop(0))

    for k in range(CHUNKS):
        cols = slice(k * BLOCK, (k + 1) * BLOCK)
        for i in range(FEAT // BLOCK):
            rows = slice(i * BLOCK, (i + 1) * BLOCK)
            keep = mask[i, k].astype(F32)
            gate_grad[rows, cols] = acc[k, rows, :BLOCK] * keep
            up_grad[rows, cols] = acc[k, rows, BLOCK:] * keep
    links.finish()
    assert len(links.ids) <= COPIES, len(links.ids)


COPIES = 220


def on_device(tokens, gate_weight, up_weight, block_mask, hidden_grad):
    vmem = pl.BlockSpec(memory_space=pltpu.VMEM)
    smem = pl.BlockSpec(memory_space=pltpu.SMEM)
    rows, width = hidden_grad.shape
    return pl.pallas_call(
        kernel,
        out_shape=(
            jax.ShapeDtypeStruct((rows, width), BF16),
            jax.ShapeDtypeStruct(gate_weight.shape, F32),
            jax.ShapeDtypeStruct(up_weight.shape, F32),
        ),
        in_specs=[vmem, vmem, vmem, smem, vmem],
        out_specs=[vmem] * 3,
        scratch_shapes=[
            pltpu.VMEM((Y, X, TOK, FEAT), BF16),
            pltpu.VMEM((Y, X // 2, TOK, FEAT), BF16),
            pltpu.VMEM((Y, FEAT, 2 * BLOCK), BF16),
            pltpu.VMEM((CHUNKS, FEAT, WIDE), BF16),
            pltpu.VMEM((CHUNKS, FEAT, WIDE), BF16),
            pltpu.VMEM((Z, CHUNKS, 2 * BLOCK, WIDE), BF16),
            pltpu.VMEM((CHUNKS, FEAT, WIDE), F32),
            pltpu.VMEM((2, len(SUMS[1]), BLOCK, WIDE), BF16),
            pltpu.VMEM((2, len(SUMS[1]), BLOCK, WIDE), BF16),
            pltpu.SemaphoreType.DMA((COPIES,)),
            pltpu.SemaphoreType.DMA((COPIES,)),
        ],
        compiler_params=pltpu.CompilerParams(
            collective_id=0, has_side_effects=True, vmem_limit_bytes=56 * 2**20
        ),
    )(tokens, gate_weight, up_weight, block_mask, hidden_grad)


def solution(mesh):
    placed = (P("col", "row"), P("row", "col"), P("row", "col"), P("row", "col"), P("row", "col"))
    return jax.shard_map(
        on_device,
        mesh=mesh,
        in_specs=placed,
        out_specs=(P("row", "col"), P("row", "col"), P("row", "col")),
        check_vma=False,
    )
```

```python
import jax
import jax.numpy as jnp
from jax import lax
from jax.experimental import pallas as pl
from jax.experimental.pallas import tpu as pltpu
from jax.sharding import PartitionSpec as P

MESH = pl.DeviceIdType.MESH
BF16, F32 = jnp.bfloat16, jnp.float32
X, Y, Z = 4, 8, 8
BLOCK = 128
TOK = 64
HALF = TOK // 2
FEAT = 512
CHUNKS = 4
WIDE = 2 * BLOCK
SCALE = 2.0**17

FIRST = {1: (0, 2), -1: (1, 3)}
NEXT = {1: (1, 0, 3, 2), -1: (0, 1, 2, 3)}
SUMS = {s: [(4, k) for k in FIRST[s]] + [(d, k) for d in (3, 2, 1) for k in NEXT[s]] for s in (1, -1)}
SIDE = {1: 0, -1: 1}
ORDER = (4, 3, -3, 2, -2, 1, -1, 0)
STEPS = """s0 s1 r0 s2 r1 f0 s3 r2 w0 S0 f1 s4 r3 f2 w1 w2 S1 s5 r4 f3 s6 r5 f4 S2 w3 w4 S3 s7 r6 f5 r7 f6 S4 t0 t1
w5 w6 S5 f7 t2 t3 S6 w7 t4 t5 t6 t7""".split()
LAST = {1: (0, 1), -1: (2, 3)}


def encode(v):
    return (v * jnp.abs(v) * (v * v)).astype(BF16)


def decode(code):
    y = code.astype(F32)
    root = lax.rsqrt(lax.rsqrt(jnp.abs(y)))
    return jnp.where(y < 0.0, -root, root)


def kernel(
    tok, gate_hbm, up_hbm, mask_hbm, cot_hbm, hidden, gate_grad, up_grad,
    gate_w, up_w, mask, cot, tall, tsib, flip, own_w, sib_w, delta, acc, sums_out, sums_in,
    load_sem, sent, got_y, got_x, got_x2, got_t, got_w, got_sum, got_delta, got_pass,
):
    row, col = lax.axis_index("row"), lax.axis_index("col")
    z, core = lax.div(row, 2), lax.rem(row, 2)
    y, x = lax.div(col, X), lax.rem(col, X)
    xs = lambda d: lax.rem(x + d + X, X)
    ys = lambda d: lax.rem(y + d + Y, Y)
    zs = lambda d: lax.rem(z + d + Z, Z)
    sibling = (z * 2 + 1 - core, col)
    xdev = {s: (row, y * X + xs(s)) for s in (1, -1)}
    ydev = {s: (row, ys(s) * X + x) for s in (1, -1)}
    zdev = {s: (zs(s) * 2 + core, col) for s in (1, -1)}

    barrier = pltpu.get_barrier_semaphore()
    partners = [sibling, *xdev.values(), *ydev.values(), *zdev.values()]
    for device in partners:
        pl.semaphore_signal(barrier, inc=1, device_id=device, device_id_type=MESH)
    loads = [(tok, tall.at[y, x]), (gate_hbm, gate_w), (up_hbm, up_w), (mask_hbm, mask), (cot_hbm, cot)]
    loads = [pltpu.make_async_copy(src, dst, load_sem.at[i]) for i, (src, dst) in enumerate(loads)]
    for load in loads:
        load.start()

    kinds = {
        "y": tall.at[pl.ds(0, Y - 1), 0],
        "x": tsib,
        "x2": tall.at[:, 0],
        "t": tsib,
        "w": own_w,
        "sum1": sums_out.at[0],
        "sum-1": sums_out.at[1],
        "delta1": sums_out.at[0],
        "delta-1": sums_out.at[1],
        "pass": delta.at[:, :, pl.ds(0, BLOCK)],
    }

    def copy(kind, src, dst, got, device):
        return pltpu.make_async_remote_copy(
            src_ref=src,
            dst_ref=dst,
            send_sem=sent.at[list(kinds).index(kind)],
            recv_sem=got,
            device_id=device,
            device_id_type=MESH,
        )

    def send(kind, src, dst, got, device):
        copy(kind, src, dst, got, device).start()

    def recv(kind, dst, got):
        copy(kind, dst, dst, got, sibling).wait_recv()

    pl.semaphore_wait(barrier, len(partners))

    part = [pl.ds(0, HALF), pl.ds(HALF, HALF)]
    half = {1: 0, -1: 1}
    mine, other = pl.ds(2 * core, 2), pl.ds(2 * (1 - core), 2)
    number = lambda s, d, p: (d - 1) * 2 + p if d < 4 else 6

    def send_x(level, src):
        for s in (1, -1):
            send("x", src, tall.at[level, x], got_x.at[SIDE[s], level], xdev[s])

    for p in (0, 1):
        for s in (1, -1):
            send("y", tok.at[part[p]], tall.at[y, x, part[p]], got_y.at[SIDE[s], number(s, 1, p)], ydev[s])
    send_x(y, tok)

    def relay_x(level):
        for s in (1, -1):
            recv("x", tall.at[level, xs(-s)], got_x.at[SIDE[s], level])
            ref = tall.at[level, xs(-s), part[half[s]]]
            send("x2", ref, ref, got_x2.at[level], xdev[s])

    def whole(level):
        recv("x2", tall.at[level, xs(2)], got_x2.at[level])
        send("t", tall.at[level, other], tsib.at[level], got_t.at[level], sibling)

    for d in (1, 2, 3, 4):
        for p in (0, 1):
            for s in (1, -1):
                if d < 4 or p == half[s]:
                    ref = tall.at[ys(-d * s), x, part[p]]
                    recv("y", ref, got_y.at[SIDE[s], number(s, d, p)])
                    if d < 3 or d == 3 and p == half[s]:
                        send("y", ref, ref, got_y.at[SIDE[s], number(s, d + 1, p)], ydev[s])
        if d < 3:
            for s in (1, -1):
                send_x(ys(-d * s), tall.at[ys(-d * s), x])
        if d == 1:
            for load in loads:
                load.wait()
            for i in range(FEAT // BLOCK):
                rows = slice(i * BLOCK, (i + 1) * BLOCK)
                for k in range(CHUNKS):
                    cols = slice(k * BLOCK, (k + 1) * BLOCK)
                    keep = mask[i, k].astype(F32) * SCALE
                    own_w[k, rows, :BLOCK] = (gate_w[rows, cols].astype(F32) * keep).astype(BF16)
                    own_w[k, rows, BLOCK:] = (up_w[rows, cols].astype(F32) * keep).astype(BF16)
            send("w", own_w, sib_w, got_w.at[0], sibling)
        if d == 2:
            relay_x(y)
        if d == 3:
            relay_x(ys(-1))
            relay_x(ys(1))
            whole(y)

    def partial(level, k):
        own = tall[level, mine].reshape(BLOCK, FEAT)
        sib = tsib[level].reshape(BLOCK, FEAT)
        return jnp.dot(own, own_w[k], preferred_element_type=F32) + jnp.dot(sib, sib_w[k], preferred_element_type=F32)

    slots = {s: {dk: i for i, dk in enumerate(SUMS[s])} for s in (1, -1)}

    def arrived(s, d, k):
        i = slots[s][d, k]
        recv(f"sum{s}", sums_in.at[SIDE[s], i], got_sum.at[SIDE[s], i])
        return decode(sums_in[SIDE[s], i])

    def sum_step(i):
        for s in (1, -1):
            d, k = SUMS[s][i]
            total = partial(zs(d * s), k)
            if d < 4 and (d + 1, k) in slots[s]:
                total += arrived(s, d + 1, k)
            sums_out[SIDE[s], i] = encode(total)
            send(f"sum{s}", sums_out.at[SIDE[s], i], sums_in.at[SIDE[s], i], got_sum.at[SIDE[s], i], zdev[s])

    for step in STEPS:
        do, n = step[0], int(step[1:])
        level = zs(ORDER[n])
        away = lax.rem(level - y + Y, Y)
        if do == "s":

            @pl.when((away >= 3) & (away <= Y - 3))
            def _():
                send_x(level, tall.at[level, x])
        elif do == "r":

            @pl.when((away >= 2) & (away <= Y - 2))
            def _():
                relay_x(level)
        elif do == "f":

            @pl.when(away >= 1)
            def _():
                whole(level)
        elif do == "w":
            recv("t", tsib.at[level], got_t.at[level])
            if n == 0:
                recv("w", sib_w, got_w.at[0])
        elif do == "S":
            sum_step(2 * n)
            sum_step(2 * n + 1)
        else:
            flip[level, :, :BLOCK] = jnp.transpose(tall[level, mine].reshape(BLOCK, FEAT))
            flip[level, :, BLOCK:] = jnp.transpose(tall[level, other].reshape(BLOCK, FEAT))

    low, high = pl.ds(0, BLOCK), pl.ds(BLOCK, BLOCK)

    def send_delta(s, d, k, ref):
        i = (d - 1) * CHUNKS + (k if d < 4 else LAST[s].index(k))
        send(f"delta{s}", ref, ref, got_delta.at[SIDE[s], i], zdev[s])

    def pass_on(n, level, k):
        send("pass", delta.at[level, k, low], delta.at[level, k, high], got_pass.at[n + 4, k], sibling)

    for k in range(CHUNKS):
        both = (partial(z, k) + arrived(1, 1, k) + arrived(-1, 1, k)) * (1.0 / SCALE)
        cols = slice(k * BLOCK, (k + 1) * BLOCK)
        gate, up = both[:, :BLOCK], both[:, BLOCK:]
        sig = 1.0 / (1.0 + jnp.exp(-gate))
        silu = gate * sig
        back = cot[:, cols].astype(F32)
        hidden[:, cols] = (silu * up).astype(BF16)
        delta[z, k, :BLOCK, :BLOCK] = (back * up * sig * (1.0 + gate * (1.0 - sig))).astype(BF16)
        delta[z, k, :BLOCK, BLOCK:] = (back * silu).astype(BF16)
        for s in (1, -1):
            send_delta(s, 1, k, delta.at[z, k, low])
        pass_on(0, z, k)

    def add(n, level, k):
        recv("pass", delta.at[level, k, high], got_pass.at[n + 4, k])
        term = jnp.dot(flip[level], delta[level, k], preferred_element_type=F32)
        acc[k] = term if n == 0 else acc[k] + term

    waiting = [(0, z, k) for k in range(CHUNKS)]
    for d in (1, 2, 3, 4):
        for k in range(CHUNKS):
            later = []
            for s in (1, -1):
                if d == 4 and k not in LAST[s]:
                    continue
                level = zs(-d * s)
                ref = delta.at[level, k, low]
                i = (d - 1) * CHUNKS + (k if d < 4 else LAST[s].index(k))
                recv(f"delta{s}", ref, got_delta.at[SIDE[s], i])
                if d < 3 or d == 3 and k in LAST[s]:
                    send_delta(s, d + 1, k, ref)
                n = d * s if d < 4 else -4
                pass_on(n, level, k)
                later.append((n, level, k))
            while len(waiting) > (3 if d < 4 else 0):
                add(*waiting.pop(0))
            waiting += later
    while waiting:
        add(*waiting.pop(0))

    for k in range(CHUNKS):
        cols = slice(k * BLOCK, (k + 1) * BLOCK)
        for i in range(FEAT // BLOCK):
            rows = slice(i * BLOCK, (i + 1) * BLOCK)
            keep = mask[i, k].astype(F32)
            gate_grad[rows, cols] = acc[k, rows, :BLOCK] * keep
            up_grad[rows, cols] = acc[k, rows, BLOCK:] * keep
    for kind, ref in kinds.items():
        copy(kind, ref, ref, got_w.at[0], sibling).wait_send()


def put_out(a, b, c, a_out, b_out, c_out, sems):
    copies = [pltpu.make_async_copy(src, dst, sems.at[i]) for i, (src, dst) in enumerate([(a, a_out), (b, b_out), (c, c_out)])]
    for copy in copies:
        copy.start()
    for copy in copies:
        copy.wait()


def on_device(tokens, gate_weight, up_weight, block_mask, hidden_grad):
    hbm = pl.BlockSpec(memory_space=pltpu.HBM)
    vmem = pl.BlockSpec(memory_space=pltpu.VMEM)
    dma = pltpu.SemaphoreType.DMA
    n_sums = len(SUMS[1])
    results = pl.pallas_call(
        kernel,
        out_shape=(
            pltpu.VMEM(hidden_grad.shape, BF16),
            pltpu.VMEM(gate_weight.shape, F32),
            pltpu.VMEM(up_weight.shape, F32),
        ),
        in_specs=[hbm] * 5,
        out_specs=[vmem] * 3,
        scratch_shapes=[
            pltpu.VMEM((FEAT, FEAT), BF16),
            pltpu.VMEM((FEAT, FEAT), BF16),
            pltpu.SMEM((FEAT // BLOCK, CHUNKS), jnp.int32),
            pltpu.VMEM((BLOCK, FEAT), BF16),
            pltpu.VMEM((Y, X, TOK, FEAT), BF16),
            pltpu.VMEM((Y, X // 2, TOK, FEAT), BF16),
            pltpu.VMEM((Y, FEAT, 2 * BLOCK), BF16),
            pltpu.VMEM((CHUNKS, FEAT, WIDE), BF16),
            pltpu.VMEM((CHUNKS, FEAT, WIDE), BF16),
            pltpu.VMEM((Z, CHUNKS, 2 * BLOCK, WIDE), BF16),
            pltpu.VMEM((CHUNKS, FEAT, WIDE), F32),
            pltpu.VMEM((2, n_sums, BLOCK, WIDE), BF16),
            pltpu.VMEM((2, n_sums, BLOCK, WIDE), BF16),
            dma((5,)), dma((10,)), dma((2, 7)), dma((2, Y)), dma((Y,)), dma((Y,)), dma((1,)),
            dma((2, n_sums)), dma((2, n_sums)), dma((Z, CHUNKS)),
        ],
        compiler_params=pltpu.CompilerParams(
            collective_id=0, has_side_effects=True, vmem_limit_bytes=60 * 2**20
        ),
    )(tokens, gate_weight, up_weight, block_mask, hidden_grad)
    anywhere = pl.BlockSpec(memory_space=pl.ANY)
    return pl.pallas_call(
        put_out,
        out_shape=[jax.ShapeDtypeStruct(r.shape, r.dtype) for r in results],
        in_specs=[anywhere] * 3,
        out_specs=[hbm] * 3,
        scratch_shapes=[dma((3,))],
        compiler_params=pltpu.CompilerParams(vmem_limit_bytes=2**20),
    )(*results)


def solution(mesh):
    placed = (P("col", "row"), P("row", "col"), P("row", "col"), P("row", "col"), P("row", "col"))
    return jax.shard_map(
        on_device,
        mesh=mesh,
        in_specs=placed,
        out_specs=(P("row", "col"), P("row", "col"), P("row", "col")),
        check_vma=False,
    )
```

```python
import jax
import jax.numpy as jnp
from jax import lax
from jax.experimental import pallas as pl
from jax.experimental.pallas import tpu as pltpu
from jax.sharding import PartitionSpec as P

MESH = pl.DeviceIdType.MESH
BF16, F32 = jnp.bfloat16, jnp.float32
X, Y, Z = 4, 8, 8
BLOCK = 128
TOK = 64
HALF = TOK // 2
PIECES = 2
FEAT = 512
CHUNKS = 4
WIDE = 2 * BLOCK
SCALE = 2.0**17

FIRST = {1: (0, 2), -1: (1, 3)}
NEXT = {1: (1, 0, 3, 2), -1: (0, 1, 2, 3)}
SUMS = {s: [(4, k) for k in FIRST[s]] + [(d, k) for d in (3, 2, 1) for k in NEXT[s]] for s in (1, -1)}
SIDE = {1: 0, -1: 1}
ORDER = (4, 3, -3, 2, -2, 1, -1, 0)
FIRST_STEPS = ("r0", "r1", "r2", "r3", "r4", "f0", "w0", "S0", "r5", "r6", "r7", "f1", "f2", "w1", "w2", "S1", "f3", "f4", "S2")
FIRST_STEPS_0 = ("r1", "r2", "r0", "r3", "r4", "f1", "f2", "w1", "w2", "A0", "r5", "r6", "r7", "f0", "w0", "A1", "f3", "f4", "A2")
STEPS = ("w3", "w4", "S3", "f5", "f6", "S4", "t0", "t1", "w5", "w6", "S5", "f7", "t2", "t3", "S6", "w7", "t4", "t5", "t6", "t7")
EARLY = {1: [(3, 1), (3, 3), (4, 0), (4, 2), (3, 0), (3, 2)], -1: [(3, 0), (3, 2), (4, 1), (4, 3), (3, 1), (3, 3)]}
LAST = {1: (0, 1), -1: (2, 3)}


def encode(v):
    return (v * jnp.abs(v) * (v * v)).astype(BF16)


def decode(code):
    y = code.astype(F32)
    root = lax.rsqrt(lax.rsqrt(jnp.abs(y)))
    return jnp.where(y < 0.0, -root, root)


def kernel(
    tok, gate_hbm, up_hbm, mask_hbm, cot_hbm, hidden, gate_grad, up_grad,
    gate_w, up_w, mask, cot, tall, tsib, flip, own_w, sib_w, delta, acc, sums_out, sums_in,
    load_sem, sent, got_y, got_x, got_x2, got_t, got_w, got_sum, got_delta, got_pass,
):
    row, col = lax.axis_index("row"), lax.axis_index("col")
    z, core = lax.div(row, 2), lax.rem(row, 2)
    y, x = lax.div(col, X), lax.rem(col, X)
    xs = lambda d: lax.rem(x + d + X, X)
    ys = lambda d: lax.rem(y + d + Y, Y)
    zs = lambda d: lax.rem(z + d + Z, Z)
    sibling = (z * 2 + 1 - core, col)
    xdev = {s: (row, y * X + xs(s)) for s in (1, -1)}
    ydev = {s: (row, ys(s) * X + x) for s in (1, -1, 2, -2)}
    zdev = {s: (zs(s) * 2 + core, col) for s in (1, -1)}

    barrier = pltpu.get_barrier_semaphore()
    partners = [sibling, *xdev.values(), *ydev.values(), *zdev.values()]
    for device in partners:
        pl.semaphore_signal(barrier, inc=1, device_id=device, device_id_type=MESH)
    loads = [(tok, tall.at[y, x]), (gate_hbm, gate_w), (up_hbm, up_w), (mask_hbm, mask), (cot_hbm, cot)]
    loads = [pltpu.make_async_copy(src, dst, load_sem.at[i]) for i, (src, dst) in enumerate(loads)]
    for load in loads:
        load.start()

    kinds = {
        "y": tall.at[pl.ds(0, Y - 1), 0],
        "x": tsib,
        "x2": tall.at[:, 0],
        "t": tsib,
        "w": own_w,
        "sum1": sums_out.at[0],
        "sum-1": sums_out.at[1],
        "delta1": sums_out.at[0],
        "delta-1": sums_out.at[1],
        "pass": delta.at[:, :, pl.ds(0, BLOCK)],
    }

    def copy(kind, src, dst, got, device):
        return pltpu.make_async_remote_copy(
            src_ref=src,
            dst_ref=dst,
            send_sem=sent.at[list(kinds).index(kind)],
            recv_sem=got,
            device_id=device,
            device_id_type=MESH,
        )

    def send(kind, src, dst, got, device):
        copy(kind, src, dst, got, device).start()

    def recv(kind, dst, got):
        copy(kind, dst, dst, got, sibling).wait_recv()

    pl.semaphore_wait(barrier, len(partners))

    part = [pl.ds(p * TOK // PIECES, TOK // PIECES) for p in range(PIECES)]
    half = {1: pl.ds(0, HALF), -1: pl.ds(HALF, HALF)}
    opposite = {1: range(PIECES // 2), -1: range(PIECES // 2, PIECES)}
    mine, other = pl.ds(2 * core, 2), pl.ds(2 * (1 - core), 2)
    number = lambda s, d, p: (d - 1) * PIECES + (p if d < 4 else p % (PIECES // 2))

    def send_x(level, src):
        for s in (1, -1):
            send("x", src, tall.at[level, x], got_x.at[SIDE[s], level], xdev[s])
        tell_sibling(level, x, src)

    def tell_sibling(level, column, src):
        @pl.when(lax.div(column, 2) != core)
        def _():
            send("t", src, tsib.at[level, lax.rem(column, 2)], got_t.at[level], sibling)

    for d in (1, 2):
        for p in range(PIECES):
            for s in (1, -1):
                send("y", tok.at[part[p]], tall.at[y, x, part[p]], got_y.at[SIDE[s], number(s, d, p)], ydev[d * s])
    send_x(y, tok)

    def relay_x(level):
        for s in (1, -1):
            recv("x", tall.at[level, xs(-s)], got_x.at[SIDE[s], level])
            ref = tall.at[level, xs(-s), half[s]]
            send("x2", ref, ref, got_x2.at[level], xdev[s])
        for s in (1, -1):
            tell_sibling(level, xs(-s), tall.at[level, xs(-s)])

    def whole(level):
        recv("x2", tall.at[level, xs(2)], got_x2.at[level])
        tell_sibling(level, xs(2), tall.at[level, xs(2)])

    for d in (1, 2, 3, 4):
        for p in range(PIECES):
            for s in (1, -1):
                if d < 4 or p in opposite[s]:
                    ref = tall.at[ys(-d * s), x, part[p]]
                    recv("y", ref, got_y.at[SIDE[s], number(s, d, p)])
                    if d == 1 or d == 2 and p in opposite[s]:
                        send("y", ref, ref, got_y.at[SIDE[s], number(s, d + 2, p)], ydev[2 * s])
        for s in (1, -1) if d < 4 else (1,):
            send_x(ys(-d * s), tall.at[ys(-d * s), x])
        if d == 1:
            for load in loads:
                load.wait()
            for i in range(FEAT // BLOCK):
                rows = slice(i * BLOCK, (i + 1) * BLOCK)
                for k in range(CHUNKS):
                    cols = slice(k * BLOCK, (k + 1) * BLOCK)
                    keep = mask[i, k].astype(F32) * SCALE
                    own_w[k, rows, :BLOCK] = (gate_w[rows, cols].astype(F32) * keep).astype(BF16)
                    own_w[k, rows, BLOCK:] = (up_w[rows, cols].astype(F32) * keep).astype(BF16)
            send("w", own_w, sib_w, got_w.at[0], sibling)

    def partial(level, k):
        own = tall[level, mine].reshape(BLOCK, FEAT)
        sib = tsib[level].reshape(BLOCK, FEAT)
        return jnp.dot(own, own_w[k], preferred_element_type=F32) + jnp.dot(sib, sib_w[k], preferred_element_type=F32)

    slots = {s: {dk: i for i, dk in enumerate(SUMS[s])} for s in (1, -1)}

    def arrived(s, d, k):
        i = slots[s][d, k]
        recv(f"sum{s}", sums_in.at[SIDE[s], i], got_sum.at[SIDE[s], i])
        return decode(sums_in[SIDE[s], i])

    def sum_step(order, i):
        for s in (1, -1):
            d, k = order[s][i]
            total = partial(zs(d * s), k)
            if d < 4 and (d + 1, k) in slots[s]:
                total += arrived(s, d + 1, k)
            i_out = slots[s][d, k]
            sums_out[SIDE[s], i_out] = encode(total)
            send(f"sum{s}", sums_out.at[SIDE[s], i_out], sums_in.at[SIDE[s], i_out], got_sum.at[SIDE[s], i_out], zdev[s])

    def take(step):
        do, n = step[0], int(step[1:])
        level = zs(ORDER[n])
        if do == "r":
            relay_x(level)
        elif do == "f":
            whole(level)
        elif do == "w":
            recv("t", tsib.at[level], got_t.at[level])
        elif do in "SA":
            for i in (2 * n, 2 * n + 1):
                sum_step(SUMS if do == "S" else EARLY, i)
        else:
            flip[level, :, :BLOCK] = jnp.transpose(tall[level, mine].reshape(BLOCK, FEAT))
            flip[level, :, BLOCK:] = jnp.transpose(tall[level, other].reshape(BLOCK, FEAT))

    recv("w", sib_w, got_w.at[0])

    @pl.when(z == y)
    def _():
        for step in FIRST_STEPS_0:
            take(step)

    @pl.when(z != y)
    def _():
        for step in FIRST_STEPS:
            take(step)

    for step in STEPS:
        take(step)

    low, high = pl.ds(0, BLOCK), pl.ds(BLOCK, BLOCK)

    def send_delta(s, d, k, ref):
        i = (d - 1) * CHUNKS + (k if d < 4 else LAST[s].index(k))
        send(f"delta{s}", ref, ref, got_delta.at[SIDE[s], i], zdev[s])

    def pass_on(n, level, k):
        send("pass", delta.at[level, k, low], delta.at[level, k, high], got_pass.at[n + 4, k], sibling)

    for k in range(CHUNKS):
        both = (partial(z, k) + arrived(1, 1, k) + arrived(-1, 1, k)) * (1.0 / SCALE)
        cols = slice(k * BLOCK, (k + 1) * BLOCK)
        gate, up = both[:, :BLOCK], both[:, BLOCK:]
        sig = 1.0 / (1.0 + jnp.exp(-gate))
        silu = gate * sig
        back = cot[:, cols].astype(F32)
        hidden[:, cols] = (silu * up).astype(BF16)
        delta[z, k, :BLOCK, :BLOCK] = (back * up * sig * (1.0 + gate * (1.0 - sig))).astype(BF16)
        delta[z, k, :BLOCK, BLOCK:] = (back * silu).astype(BF16)
        for s in (1, -1):
            send_delta(s, 1, k, delta.at[z, k, low])
        pass_on(0, z, k)

    def add(n, level, k):
        recv("pass", delta.at[level, k, high], got_pass.at[n + 4, k])
        term = jnp.dot(flip[level], delta[level, k], preferred_element_type=F32)
        acc[k] = term if n == 0 else acc[k] + term

    waiting = [(0, z, k) for k in range(CHUNKS)]
    for d in (1, 2, 3, 4):
        for k in range(CHUNKS):
            later = []
            for s in (1, -1):
                if d == 4 and k not in LAST[s]:
                    continue
                level = zs(-d * s)
                ref = delta.at[level, k, low]
                i = (d - 1) * CHUNKS + (k if d < 4 else LAST[s].index(k))
                recv(f"delta{s}", ref, got_delta.at[SIDE[s], i])
                if d < 3 or d == 3 and k in LAST[s]:
                    send_delta(s, d + 1, k, ref)
                n = d * s if d < 4 else -4
                pass_on(n, level, k)
                later.append((n, level, k))
            while len(waiting) > (3 if d < 4 else 0):
                add(*waiting.pop(0))
            waiting += later
    while waiting:
        add(*waiting.pop(0))

    for k in range(CHUNKS):
        cols = slice(k * BLOCK, (k + 1) * BLOCK)
        for i in range(FEAT // BLOCK):
            rows = slice(i * BLOCK, (i + 1) * BLOCK)
            keep = mask[i, k].astype(F32)
            gate_grad[rows, cols] = acc[k, rows, :BLOCK] * keep
            up_grad[rows, cols] = acc[k, rows, BLOCK:] * keep
    for kind, ref in kinds.items():
        copy(kind, ref, ref, got_w.at[0], sibling).wait_send()


def put_out(a, b, c, a_out, b_out, c_out, sems):
    copies = [pltpu.make_async_copy(src, dst, sems.at[i]) for i, (src, dst) in enumerate([(a, a_out), (b, b_out), (c, c_out)])]
    for copy in copies:
        copy.start()
    for copy in copies:
        copy.wait()


def on_device(tokens, gate_weight, up_weight, block_mask, hidden_grad):
    hbm = pl.BlockSpec(memory_space=pltpu.HBM)
    vmem = pl.BlockSpec(memory_space=pltpu.VMEM)
    dma = pltpu.SemaphoreType.DMA
    n_sums = len(SUMS[1])
    results = pl.pallas_call(
        kernel,
        out_shape=(
            pltpu.VMEM(hidden_grad.shape, BF16),
            pltpu.VMEM(gate_weight.shape, F32),
            pltpu.VMEM(up_weight.shape, F32),
        ),
        in_specs=[hbm] * 5,
        out_specs=[vmem] * 3,
        scratch_shapes=[
            pltpu.VMEM((FEAT, FEAT), BF16),
            pltpu.VMEM((FEAT, FEAT), BF16),
            pltpu.SMEM((FEAT // BLOCK, CHUNKS), jnp.int32),
            pltpu.VMEM((BLOCK, FEAT), BF16),
            pltpu.VMEM((Y, X, TOK, FEAT), BF16),
            pltpu.VMEM((Y, X // 2, TOK, FEAT), BF16),
            pltpu.VMEM((Y, FEAT, 2 * BLOCK), BF16),
            pltpu.VMEM((CHUNKS, FEAT, WIDE), BF16),
            pltpu.VMEM((CHUNKS, FEAT, WIDE), BF16),
            pltpu.VMEM((Z, CHUNKS, 2 * BLOCK, WIDE), BF16),
            pltpu.VMEM((CHUNKS, FEAT, WIDE), F32),
            pltpu.VMEM((2, n_sums, BLOCK, WIDE), BF16),
            pltpu.VMEM((2, n_sums, BLOCK, WIDE), BF16),
            dma((5,)), dma((10,)), dma((2, 7 * PIECES // 2)), dma((2, Y)), dma((Y,)), dma((Y,)), dma((1,)),
            dma((2, n_sums)), dma((2, n_sums)), dma((Z, CHUNKS)),
        ],
        compiler_params=pltpu.CompilerParams(
            collective_id=0, has_side_effects=True, vmem_limit_bytes=60 * 2**20
        ),
    )(tokens, gate_weight, up_weight, block_mask, hidden_grad)
    anywhere = pl.BlockSpec(memory_space=pl.ANY)
    return pl.pallas_call(
        put_out,
        out_shape=[jax.ShapeDtypeStruct(r.shape, r.dtype) for r in results],
        in_specs=[anywhere] * 3,
        out_specs=[hbm] * 3,
        scratch_shapes=[dma((3,))],
        compiler_params=pltpu.CompilerParams(vmem_limit_bytes=2**20),
    )(*results)


def solution(mesh):
    placed = (P("col", "row"), P("row", "col"), P("row", "col"), P("row", "col"), P("row", "col"))
    return jax.shard_map(
        on_device,
        mesh=mesh,
        in_specs=placed,
        out_specs=(P("row", "col"), P("row", "col"), P("row", "col")),
        check_vma=False,
    )
```

```python
import jax
import jax.numpy as jnp
from jax import lax
from jax.experimental import pallas as pl
from jax.experimental.pallas import tpu as pltpu
from jax.sharding import PartitionSpec as P

MESH = pl.DeviceIdType.MESH
BF16, F32 = jnp.bfloat16, jnp.float32
X, Y, Z = 4, 8, 8
BLOCK = 128
TOK = 64
HALF = TOK // 2
PIECES = 2
FEAT = 512
CHUNKS = 4
WIDE = 2 * BLOCK
SCALE = 2.0**17

FIRST = {1: (0, 2), -1: (1, 3)}
NEXT = {1: (1, 0, 3, 2), -1: (0, 1, 2, 3)}
SUMS = {s: [(4, k) for k in FIRST[s]] + [(d, k) for d in (3, 2, 1) for k in NEXT[s]] for s in (1, -1)}
SIDE = {1: 0, -1: 1}
ORDER = (4, 3, -3, 2, -2, 1, -1, 0)
FIRST_STEPS = ("r0", "r1", "r2", "r3", "r4", "f0", "w0", "S0", "r5", "r6", "r7", "f1", "f2", "w1", "w2", "S1", "f3", "f4", "S2")
STEPS = ("w3", "w4", "S3", "f5", "f6", "S4", "t0", "t1", "w5", "w6", "S5", "f7", "t2", "t3", "S6", "w7", "t4", "t5", "t6", "t7")
LAST = {1: (0, 1), -1: (2, 3)}


def encode(v):
    return (v * jnp.abs(v) * (v * v)).astype(BF16)


def decode(code):
    y = code.astype(F32)
    root = lax.rsqrt(lax.rsqrt(jnp.abs(y)))
    return jnp.where(y < 0.0, -root, root)


def kernel(
    tok, gate_hbm, up_hbm, mask_hbm, cot_hbm, hidden, gate_grad, up_grad,
    gate_w, up_w, mask, cot, tall, tsib, flip, own_w, sib_w, delta, acc, sums_out, sums_in,
    load_sem, sent, got_y, got_x, got_x2, got_t, got_w, got_sum, got_delta, got_pass,
):
    row, col = lax.axis_index("row"), lax.axis_index("col")
    z, core = lax.div(row, 2), lax.rem(row, 2)
    y, x = lax.div(col, X), lax.rem(col, X)
    xs = lambda d: lax.rem(x + d + X, X)
    ys = lambda d: lax.rem(y + d + Y, Y)
    zs = lambda d: lax.rem(z + d + Z, Z)
    sibling = (z * 2 + 1 - core, col)
    xdev = {s: (row, y * X + xs(s)) for s in (1, -1)}
    ydev = {s: (row, ys(s) * X + x) for s in (1, -1, 2, -2)}
    zdev = {s: (zs(s) * 2 + core, col) for s in (1, -1)}

    barrier = pltpu.get_barrier_semaphore()
    partners = [sibling, *xdev.values(), *ydev.values(), *zdev.values()]
    for device in partners:
        pl.semaphore_signal(barrier, inc=1, device_id=device, device_id_type=MESH)
    loads = [(tok, tall.at[y, x]), (gate_hbm, gate_w), (up_hbm, up_w), (mask_hbm, mask), (cot_hbm, cot)]
    loads = [pltpu.make_async_copy(src, dst, load_sem.at[i]) for i, (src, dst) in enumerate(loads)]
    for load in loads:
        load.start()

    kinds = {
        "y": tall.at[pl.ds(0, Y - 1), 0],
        "x": tsib,
        "x2": tall.at[:, 0],
        "t": tsib,
        "w": own_w,
        "sum1": sums_out.at[0],
        "sum-1": sums_out.at[1],
        "delta1": sums_out.at[0],
        "delta-1": sums_out.at[1],
        "pass": delta.at[:, :, pl.ds(0, BLOCK)],
    }

    def copy(kind, src, dst, got, device):
        return pltpu.make_async_remote_copy(
            src_ref=src,
            dst_ref=dst,
            send_sem=sent.at[list(kinds).index(kind)],
            recv_sem=got,
            device_id=device,
            device_id_type=MESH,
        )

    def send(kind, src, dst, got, device):
        copy(kind, src, dst, got, device).start()

    def recv(kind, dst, got):
        copy(kind, dst, dst, got, sibling).wait_recv()

    pl.semaphore_wait(barrier, len(partners))

    part = [pl.ds(p * TOK // PIECES, TOK // PIECES) for p in range(PIECES)]
    half = {1: pl.ds(0, HALF), -1: pl.ds(HALF, HALF)}
    opposite = {1: range(PIECES // 2), -1: range(PIECES // 2, PIECES)}
    mine, other = pl.ds(2 * core, 2), pl.ds(2 * (1 - core), 2)
    number = lambda s, d, p: (d - 1) * PIECES + (p if d < 4 else p % (PIECES // 2))

    def send_x(level, src):
        for s in (1, -1):
            send("x", src, tall.at[level, x], got_x.at[SIDE[s], level], xdev[s])
        tell_sibling(level, x, src)

    def tell_sibling(level, column, src):
        @pl.when(lax.div(column, 2) != core)
        def _():
            send("t", src, tsib.at[level, lax.rem(column, 2)], got_t.at[level], sibling)

    for d in (1, 2):
        for p in range(PIECES):
            for s in (1, -1):
                send("y", tok.at[part[p]], tall.at[y, x, part[p]], got_y.at[SIDE[s], number(s, d, p)], ydev[d * s])
    send_x(y, tok)

    def relay_x(level):
        for s in (1, -1):
            recv("x", tall.at[level, xs(-s)], got_x.at[SIDE[s], level])
            ref = tall.at[level, xs(-s), half[s]]
            send("x2", ref, ref, got_x2.at[level], xdev[s])
        for s in (1, -1):
            tell_sibling(level, xs(-s), tall.at[level, xs(-s)])

    def whole(level):
        recv("x2", tall.at[level, xs(2)], got_x2.at[level])
        tell_sibling(level, xs(2), tall.at[level, xs(2)])

    away = lax.rem(z - y + Y, Y)
    for d in (1, 2, 3, 4):
        for p in range(PIECES):
            for s in (1, -1):
                if d < 4 or p in opposite[s]:
                    ref = tall.at[ys(-d * s), x, part[p]]
                    recv("y", ref, got_y.at[SIDE[s], number(s, d, p)])
                    if d == 1 or d == 2 and p in opposite[s]:
                        send("y", ref, ref, got_y.at[SIDE[s], number(s, d + 2, p)], ydev[2 * s])
        if d < 3:
            for s in (1, -1):
                send_x(ys(-d * s), tall.at[ys(-d * s), x])
        elif d == 3:
            for turn, order in ((Y - 1, (3, -3)), (None, (-3, 3))):
                now = (away != 0) & (away != Y - 1) if turn is None else away == turn

                @pl.when(now)
                def _():
                    for dy in order:
                        send_x(ys(dy), tall.at[ys(dy), x])
        else:
            send_x(ys(4), tall.at[ys(4), x])

            @pl.when(away == 0)
            def _():
                for dy in (-3, 3):
                    send_x(ys(dy), tall.at[ys(dy), x])
        if d == 1:
            for load in loads:
                load.wait()
            for i in range(FEAT // BLOCK):
                rows = slice(i * BLOCK, (i + 1) * BLOCK)
                for k in range(CHUNKS):
                    cols = slice(k * BLOCK, (k + 1) * BLOCK)
                    keep = mask[i, k].astype(F32) * SCALE
                    own_w[k, rows, :BLOCK] = (gate_w[rows, cols].astype(F32) * keep).astype(BF16)
                    own_w[k, rows, BLOCK:] = (up_w[rows, cols].astype(F32) * keep).astype(BF16)
            send("w", own_w, sib_w, got_w.at[0], sibling)

    def partial(level, k):
        own = tall[level, mine].reshape(BLOCK, FEAT)
        sib = tsib[level].reshape(BLOCK, FEAT)
        return jnp.dot(own, own_w[k], preferred_element_type=F32) + jnp.dot(sib, sib_w[k], preferred_element_type=F32)

    slots = {s: {dk: i for i, dk in enumerate(SUMS[s])} for s in (1, -1)}

    def arrived(s, d, k):
        i = slots[s][d, k]
        recv(f"sum{s}", sums_in.at[SIDE[s], i], got_sum.at[SIDE[s], i])
        return decode(sums_in[SIDE[s], i])

    def sum_step(i):
        for s in (1, -1):
            d, k = SUMS[s][i]
            total = partial(zs(d * s), k)
            if d < 4 and (d + 1, k) in slots[s]:
                total += arrived(s, d + 1, k)
            i_out = slots[s][d, k]
            sums_out[SIDE[s], i_out] = encode(total)
            send(f"sum{s}", sums_out.at[SIDE[s], i_out], sums_in.at[SIDE[s], i_out], got_sum.at[SIDE[s], i_out], zdev[s])

    def take(step):
        do, n = step[0], int(step[1:])
        level = zs(ORDER[n])
        if do == "r":
            relay_x(level)
        elif do == "f":
            whole(level)
        elif do == "w":
            recv("t", tsib.at[level], got_t.at[level])
        elif do == "S":
            for i in (2 * n, 2 * n + 1):
                sum_step(i)
        else:
            flip[level, :, :BLOCK] = jnp.transpose(tall[level, mine].reshape(BLOCK, FEAT))
            flip[level, :, BLOCK:] = jnp.transpose(tall[level, other].reshape(BLOCK, FEAT))

    recv("w", sib_w, got_w.at[0])

    for step in FIRST_STEPS:
        take(step)

    for step in STEPS:
        take(step)

    low, high = pl.ds(0, BLOCK), pl.ds(BLOCK, BLOCK)

    def send_delta(s, d, k, ref):
        i = (d - 1) * CHUNKS + (k if d < 4 else LAST[s].index(k))
        send(f"delta{s}", ref, ref, got_delta.at[SIDE[s], i], zdev[s])

    def pass_on(n, level, k):
        send("pass", delta.at[level, k, low], delta.at[level, k, high], got_pass.at[n + 4, k], sibling)

    for k in range(CHUNKS):
        both = (partial(z, k) + arrived(1, 1, k) + arrived(-1, 1, k)) * (1.0 / SCALE)
        cols = slice(k * BLOCK, (k + 1) * BLOCK)
        gate, up = both[:, :BLOCK], both[:, BLOCK:]
        sig = 1.0 / (1.0 + jnp.exp(-gate))
        silu = gate * sig
        back = cot[:, cols].astype(F32)
        hidden[:, cols] = (silu * up).astype(BF16)
        delta[z, k, :BLOCK, :BLOCK] = (back * up * sig * (1.0 + gate * (1.0 - sig))).astype(BF16)
        delta[z, k, :BLOCK, BLOCK:] = (back * silu).astype(BF16)
        for s in (1, -1):
            send_delta(s, 1, k, delta.at[z, k, low])
        pass_on(0, z, k)

    def add(n, level, k):
        recv("pass", delta.at[level, k, high], got_pass.at[n + 4, k])
        term = jnp.dot(flip[level], delta[level, k], preferred_element_type=F32)
        acc[k] = term if n == 0 else acc[k] + term

    waiting = [(0, z, k) for k in range(CHUNKS)]
    for d in (1, 2, 3, 4):
        for k in range(CHUNKS):
            later = []
            for s in (1, -1):
                if d == 4 and k not in LAST[s]:
                    continue
                level = zs(-d * s)
                ref = delta.at[level, k, low]
                i = (d - 1) * CHUNKS + (k if d < 4 else LAST[s].index(k))
                recv(f"delta{s}", ref, got_delta.at[SIDE[s], i])
                if d < 3 or d == 3 and k in LAST[s]:
                    send_delta(s, d + 1, k, ref)
                n = d * s if d < 4 else -4
                pass_on(n, level, k)
                later.append((n, level, k))
            while len(waiting) > (3 if d < 4 else 0):
                add(*waiting.pop(0))
            waiting += later
    while waiting:
        add(*waiting.pop(0))

    for k in range(CHUNKS):
        cols = slice(k * BLOCK, (k + 1) * BLOCK)
        for i in range(FEAT // BLOCK):
            rows = slice(i * BLOCK, (i + 1) * BLOCK)
            keep = mask[i, k].astype(F32)
            gate_grad[rows, cols] = acc[k, rows, :BLOCK] * keep
            up_grad[rows, cols] = acc[k, rows, BLOCK:] * keep
    for kind, ref in kinds.items():
        copy(kind, ref, ref, got_w.at[0], sibling).wait_send()


def put_out(a, b, c, a_out, b_out, c_out, sems):
    copies = [pltpu.make_async_copy(src, dst, sems.at[i]) for i, (src, dst) in enumerate([(a, a_out), (b, b_out), (c, c_out)])]
    for copy in copies:
        copy.start()
    for copy in copies:
        copy.wait()


def on_device(tokens, gate_weight, up_weight, block_mask, hidden_grad):
    hbm = pl.BlockSpec(memory_space=pltpu.HBM)
    vmem = pl.BlockSpec(memory_space=pltpu.VMEM)
    dma = pltpu.SemaphoreType.DMA
    n_sums = len(SUMS[1])
    results = pl.pallas_call(
        kernel,
        out_shape=(
            pltpu.VMEM(hidden_grad.shape, BF16),
            pltpu.VMEM(gate_weight.shape, F32),
            pltpu.VMEM(up_weight.shape, F32),
        ),
        in_specs=[hbm] * 5,
        out_specs=[vmem] * 3,
        scratch_shapes=[
            pltpu.VMEM((FEAT, FEAT), BF16),
            pltpu.VMEM((FEAT, FEAT), BF16),
            pltpu.SMEM((FEAT // BLOCK, CHUNKS), jnp.int32),
            pltpu.VMEM((BLOCK, FEAT), BF16),
            pltpu.VMEM((Y, X, TOK, FEAT), BF16),
            pltpu.VMEM((Y, X // 2, TOK, FEAT), BF16),
            pltpu.VMEM((Y, FEAT, 2 * BLOCK), BF16),
            pltpu.VMEM((CHUNKS, FEAT, WIDE), BF16),
            pltpu.VMEM((CHUNKS, FEAT, WIDE), BF16),
            pltpu.VMEM((Z, CHUNKS, 2 * BLOCK, WIDE), BF16),
            pltpu.VMEM((CHUNKS, FEAT, WIDE), F32),
            pltpu.VMEM((2, n_sums, BLOCK, WIDE), BF16),
            pltpu.VMEM((2, n_sums, BLOCK, WIDE), BF16),
            dma((5,)), dma((10,)), dma((2, 7 * PIECES // 2)), dma((2, Y)), dma((Y,)), dma((Y,)), dma((1,)),
            dma((2, n_sums)), dma((2, n_sums)), dma((Z, CHUNKS)),
        ],
        compiler_params=pltpu.CompilerParams(
            collective_id=0, has_side_effects=True, vmem_limit_bytes=60 * 2**20
        ),
    )(tokens, gate_weight, up_weight, block_mask, hidden_grad)
    anywhere = pl.BlockSpec(memory_space=pl.ANY)
    return pl.pallas_call(
        put_out,
        out_shape=[jax.ShapeDtypeStruct(r.shape, r.dtype) for r in results],
        in_specs=[anywhere] * 3,
        out_specs=[hbm] * 3,
        scratch_shapes=[dma((3,))],
        compiler_params=pltpu.CompilerParams(vmem_limit_bytes=2**20),
    )(*results)


def solution(mesh):
    placed = (P("col", "row"), P("row", "col"), P("row", "col"), P("row", "col"), P("row", "col"))
    return jax.shard_map(
        on_device,
        mesh=mesh,
        in_specs=placed,
        out_specs=(P("row", "col"), P("row", "col"), P("row", "col")),
        check_vma=False,
    )
```

```python
import jax
import jax.numpy as jnp
from jax import lax
from jax.experimental import pallas as pl
from jax.experimental.pallas import tpu as pltpu
from jax.sharding import PartitionSpec as P

MESH = pl.DeviceIdType.MESH
BF16, F32 = jnp.bfloat16, jnp.float32
X, Y, Z = 4, 8, 8
BLOCK = 128
TOK = 64
HALF = TOK // 2
PIECES = 2
FEAT = 512
CHUNKS = 4
WIDE = 2 * BLOCK
SCALE = 2.0**17

FIRST = {1: (0, 2), -1: (1, 3)}
NEXT = {1: (1, 0, 3, 2), -1: (0, 1, 2, 3)}
SUMS = {s: [(4, k) for k in FIRST[s]] + [(d, k) for d in (3, 2, 1) for k in NEXT[s]] for s in (1, -1)}
SIDE = {1: 0, -1: 1}
ORDER = (4, 3, -3, 2, -2, 1, -1, 0)
FIRST_STEPS = ("r0", "r1", "r2", "r3", "r4", "f0", "w0", "S0", "r5", "r6", "r7", "f1", "f2", "w1", "w2", "S1", "f3", "f4", "S2")
STEPS = ("w3", "w4", "S3", "f5", "f6", "S4", "t0", "t1", "w5", "w6", "S5", "f7", "t2", "t3", "S6", "w7", "t4", "t5", "t6", "t7")
LAST = {1: (0, 1), -1: (2, 3)}


def encode(v):
    return (v * jnp.abs(v) * (v * v)).astype(BF16)


def decode(code):
    y = code.astype(F32)
    root = lax.rsqrt(lax.rsqrt(jnp.abs(y)))
    return jnp.where(y < 0.0, -root, root)


def kernel(
    tok, gate_hbm, up_hbm, mask_hbm, cot_hbm, hidden, gate_grad, up_grad,
    gate_w, up_w, mask, cot, tall, tsib, flip, own_w, sib_w, delta, acc, sums_out, sums_in,
    load_sem, sent, got_y, got_x, got_x2, got_t, got_w, got_sum, got_delta, got_pass,
):
    row, col = lax.axis_index("row"), lax.axis_index("col")
    z, core = lax.div(row, 2), lax.rem(row, 2)
    y, x = lax.div(col, X), lax.rem(col, X)
    xs = lambda d: lax.rem(x + d + X, X)
    ys = lambda d: lax.rem(y + d + Y, Y)
    zs = lambda d: lax.rem(z + d + Z, Z)
    sibling = (z * 2 + 1 - core, col)
    xdev = {s: (row, y * X + xs(s)) for s in (1, -1)}
    ydev = {s: (row, ys(s) * X + x) for s in (1, -1, 2, -2)}
    zdev = {s: (zs(s) * 2 + core, col) for s in (1, -1)}

    barrier = pltpu.get_barrier_semaphore()
    partners = [sibling, *xdev.values(), *ydev.values(), *zdev.values()]
    for device in partners:
        pl.semaphore_signal(barrier, inc=1, device_id=device, device_id_type=MESH)
    loads = [(tok, tall.at[y, x]), (gate_hbm, gate_w), (up_hbm, up_w), (mask_hbm, mask), (cot_hbm, cot)]
    loads = [pltpu.make_async_copy(src, dst, load_sem.at[i]) for i, (src, dst) in enumerate(loads)]
    for load in loads:
        load.start()

    kinds = {
        "y": tall.at[pl.ds(0, Y - 1), 0],
        "x": tsib,
        "x2": tall.at[:, 0],
        "t": tsib,
        "w": own_w,
        "sum1": sums_out.at[0],
        "sum-1": sums_out.at[1],
        "delta1": sums_out.at[0],
        "delta-1": sums_out.at[1],
        "pass": delta.at[:, :, pl.ds(0, BLOCK)],
    }

    def copy(kind, src, dst, got, device):
        return pltpu.make_async_remote_copy(
            src_ref=src,
            dst_ref=dst,
            send_sem=sent.at[list(kinds).index(kind)],
            recv_sem=got,
            device_id=device,
            device_id_type=MESH,
        )

    def send(kind, src, dst, got, device):
        copy(kind, src, dst, got, device).start()

    def recv(kind, dst, got):
        copy(kind, dst, dst, got, sibling).wait_recv()

    pl.semaphore_wait(barrier, len(partners))

    part = [pl.ds(p * TOK // PIECES, TOK // PIECES) for p in range(PIECES)]
    half = {1: pl.ds(0, HALF), -1: pl.ds(HALF, HALF)}
    opposite = {1: range(PIECES // 2), -1: range(PIECES // 2, PIECES)}
    mine, other = pl.ds(2 * core, 2), pl.ds(2 * (1 - core), 2)
    number = lambda s, d, p: (d - 1) * PIECES + (p if d < 4 else p % (PIECES // 2))

    def send_x(level, src):
        for s in (1, -1):
            send("x", src, tall.at[level, x], got_x.at[SIDE[s], level], xdev[s])
        tell_sibling(level, x, src)

    def tell_sibling(level, column, src):
        @pl.when(lax.div(column, 2) != core)
        def _():
            send("t", src, tsib.at[level, lax.rem(column, 2)], got_t.at[level], sibling)

    for d in (1, 2):
        for p in range(PIECES):
            for s in (1, -1):
                send("y", tok.at[part[p]], tall.at[y, x, part[p]], got_y.at[SIDE[s], number(s, d, p)], ydev[d * s])
    send_x(y, tok)

    def relay_x(level):
        for s in (1, -1):
            recv("x", tall.at[level, xs(-s)], got_x.at[SIDE[s], level])
            ref = tall.at[level, xs(-s), half[s]]
            send("x2", ref, ref, got_x2.at[level], xdev[s])
        for s in (1, -1):
            tell_sibling(level, xs(-s), tall.at[level, xs(-s)])

    def whole(level):
        recv("x2", tall.at[level, xs(2)], got_x2.at[level])
        tell_sibling(level, xs(2), tall.at[level, xs(2)])

    away = lax.rem(z - y + Y, Y)
    for d in (1, 2, 3, 4):
        for p in range(PIECES):
            for s in (1, -1):
                if d < 4 or p in opposite[s]:
                    ref = tall.at[ys(-d * s), x, part[p]]
                    recv("y", ref, got_y.at[SIDE[s], number(s, d, p)])
                    if d == 1 or d == 2 and p in opposite[s]:
                        send("y", ref, ref, got_y.at[SIDE[s], number(s, d + 2, p)], ydev[2 * s])
        if d < 3:
            for s in (1, -1):
                send_x(ys(-d * s), tall.at[ys(-d * s), x])
        elif d == 3:
            for turn, order in ((Y - 1, (3, -3)), (None, (-3, 3))):
                now = (away != 0) & (away != Y - 1) if turn is None else away == turn

                @pl.when(now)
                def _():
                    for dy in order:
                        send_x(ys(dy), tall.at[ys(dy), x])
        else:
            send_x(ys(4), tall.at[ys(4), x])

            @pl.when(away == 0)
            def _():
                for dy in (-3, 3):
                    send_x(ys(dy), tall.at[ys(dy), x])
        if d == 1:
            for load in loads:
                load.wait()
            for i in range(FEAT // BLOCK):
                rows = slice(i * BLOCK, (i + 1) * BLOCK)
                for k in range(CHUNKS):
                    cols = slice(k * BLOCK, (k + 1) * BLOCK)
                    keep = mask[i, k].astype(F32) * SCALE
                    own_w[k, rows, :BLOCK] = (gate_w[rows, cols].astype(F32) * keep).astype(BF16)
                    own_w[k, rows, BLOCK:] = (up_w[rows, cols].astype(F32) * keep).astype(BF16)
            send("w", own_w, sib_w, got_w.at[0], sibling)

    def partial(level, k):
        own = tall[level, mine].reshape(BLOCK, FEAT)
        sib = tsib[level].reshape(BLOCK, FEAT)
        return jnp.dot(own, own_w[k], preferred_element_type=F32) + jnp.dot(sib, sib_w[k], preferred_element_type=F32)

    slots = {s: {dk: i for i, dk in enumerate(SUMS[s])} for s in (1, -1)}

    def arrived(s, d, k):
        i = slots[s][d, k]
        recv(f"sum{s}", sums_in.at[SIDE[s], i], got_sum.at[SIDE[s], i])
        return decode(sums_in[SIDE[s], i])

    def sum_step(i):
        for s in (1, -1):
            d, k = SUMS[s][i]
            total = partial(zs(d * s), k)
            if d < 4 and (d + 1, k) in slots[s]:
                total += arrived(s, d + 1, k)
            i_out = slots[s][d, k]
            sums_out[SIDE[s], i_out] = encode(total)
            send(f"sum{s}", sums_out.at[SIDE[s], i_out], sums_in.at[SIDE[s], i_out], got_sum.at[SIDE[s], i_out], zdev[s])

    def take(step):
        do, n = step[0], int(step[1:])
        level = zs(ORDER[n])
        if do == "r":
            relay_x(level)
        elif do == "f":
            whole(level)
        elif do == "w":
            recv("t", tsib.at[level], got_t.at[level])
        elif do == "S":
            for i in (2 * n, 2 * n + 1):
                sum_step(i)
        else:
            flip[level, :, :BLOCK] = jnp.transpose(tall[level, mine].reshape(BLOCK, FEAT))
            flip[level, :, BLOCK:] = jnp.transpose(tall[level, other].reshape(BLOCK, FEAT))

    recv("w", sib_w, got_w.at[0])

    for step in FIRST_STEPS:
        take(step)

    for step in STEPS:
        take(step)

    low, high = pl.ds(0, BLOCK), pl.ds(BLOCK, BLOCK)

    def send_delta(s, d, k, ref):
        i = (d - 1) * CHUNKS + (k if d < 4 else LAST[s].index(k))
        send(f"delta{s}", ref, ref, got_delta.at[SIDE[s], i], zdev[s])

    def pass_on(n, level, k):
        send("pass", delta.at[level, k, low], delta.at[level, k, high], got_pass.at[n + 4, k], sibling)

    for k in range(CHUNKS):
        both = (partial(z, k) + arrived(1, 1, k) + arrived(-1, 1, k)) * (1.0 / SCALE)
        cols = slice(k * BLOCK, (k + 1) * BLOCK)
        gate, up = both[:, :BLOCK], both[:, BLOCK:]
        sig = 1.0 / (1.0 + jnp.exp(-gate))
        silu = gate * sig
        back = cot[:, cols].astype(F32)
        hidden[:, cols] = (silu * up).astype(BF16)
        delta[z, k, :BLOCK, :BLOCK] = (back * up * sig * (1.0 + gate * (1.0 - sig))).astype(BF16)
        delta[z, k, :BLOCK, BLOCK:] = (back * silu).astype(BF16)
        for s in (1, -1):
            send_delta(s, 1, k, delta.at[z, k, low])
        pass_on(0, z, k)

    def add(n, level, k):
        recv("pass", delta.at[level, k, high], got_pass.at[n + 4, k])
        term = jnp.dot(flip[level], delta[level, k], preferred_element_type=F32)
        acc[k] = term if n == 0 else acc[k] + term

    waiting = [(0, z, k) for k in range(CHUNKS)]
    for d in (1, 2, 3, 4):
        for k in range(CHUNKS) if d < 4 else (0, 2, 1, 3):
            later = []
            for s in (1, -1):
                if d == 4 and k not in LAST[s]:
                    continue
                level = zs(-d * s)
                ref = delta.at[level, k, low]
                i = (d - 1) * CHUNKS + (k if d < 4 else LAST[s].index(k))
                recv(f"delta{s}", ref, got_delta.at[SIDE[s], i])
                if d < 3 or d == 3 and k in LAST[s]:
                    send_delta(s, d + 1, k, ref)
                n = d * s if d < 4 else -4
                pass_on(n, level, k)
                later.append((n, level, k))
            while len(waiting) > (3 if d < 4 else 1 if k == 2 else CHUNKS + 2):
                add(*waiting.pop(0))
            waiting += later

    def store(k):
        cols = slice(k * BLOCK, (k + 1) * BLOCK)
        for i in range(FEAT // BLOCK):
            rows = slice(i * BLOCK, (i + 1) * BLOCK)
            keep = mask[i, k].astype(F32)
            gate_grad[rows, cols] = acc[k, rows, :BLOCK] * keep
            up_grad[rows, cols] = acc[k, rows, BLOCK:] * keep

    order = [w[2] for w in waiting]
    for i, k in enumerate(order):
        add(*waiting[i])
        if k not in order[i + 1 :]:
            store(k)
    for kind, ref in kinds.items():
        copy(kind, ref, ref, got_w.at[0], sibling).wait_send()


def put_out(a, b, c, a_out, b_out, c_out, sems):
    copies = [pltpu.make_async_copy(src, dst, sems.at[i]) for i, (src, dst) in enumerate([(a, a_out), (b, b_out), (c, c_out)])]
    for copy in copies:
        copy.start()
    for copy in copies:
        copy.wait()


def on_device(tokens, gate_weight, up_weight, block_mask, hidden_grad):
    hbm = pl.BlockSpec(memory_space=pltpu.HBM)
    vmem = pl.BlockSpec(memory_space=pltpu.VMEM)
    dma = pltpu.SemaphoreType.DMA
    n_sums = len(SUMS[1])
    results = pl.pallas_call(
        kernel,
        out_shape=(
            pltpu.VMEM(hidden_grad.shape, BF16),
            pltpu.VMEM(gate_weight.shape, F32),
            pltpu.VMEM(up_weight.shape, F32),
        ),
        in_specs=[hbm] * 5,
        out_specs=[vmem] * 3,
        scratch_shapes=[
            pltpu.VMEM((FEAT, FEAT), BF16),
            pltpu.VMEM((FEAT, FEAT), BF16),
            pltpu.SMEM((FEAT // BLOCK, CHUNKS), jnp.int32),
            pltpu.VMEM((BLOCK, FEAT), BF16),
            pltpu.VMEM((Y, X, TOK, FEAT), BF16),
            pltpu.VMEM((Y, X // 2, TOK, FEAT), BF16),
            pltpu.VMEM((Y, FEAT, 2 * BLOCK), BF16),
            pltpu.VMEM((CHUNKS, FEAT, WIDE), BF16),
            pltpu.VMEM((CHUNKS, FEAT, WIDE), BF16),
            pltpu.VMEM((Z, CHUNKS, 2 * BLOCK, WIDE), BF16),
            pltpu.VMEM((CHUNKS, FEAT, WIDE), F32),
            pltpu.VMEM((2, n_sums, BLOCK, WIDE), BF16),
            pltpu.VMEM((2, n_sums, BLOCK, WIDE), BF16),
            dma((5,)), dma((10,)), dma((2, 7 * PIECES // 2)), dma((2, Y)), dma((Y,)), dma((Y,)), dma((1,)),
            dma((2, n_sums)), dma((2, n_sums)), dma((Z, CHUNKS)),
        ],
        compiler_params=pltpu.CompilerParams(
            collective_id=0, has_side_effects=True, vmem_limit_bytes=60 * 2**20
        ),
    )(tokens, gate_weight, up_weight, block_mask, hidden_grad)
    anywhere = pl.BlockSpec(memory_space=pl.ANY)
    return pl.pallas_call(
        put_out,
        out_shape=[jax.ShapeDtypeStruct(r.shape, r.dtype) for r in results],
        in_specs=[anywhere] * 3,
        out_specs=[hbm] * 3,
        scratch_shapes=[dma((3,))],
        compiler_params=pltpu.CompilerParams(vmem_limit_bytes=2**20),
    )(*results)


def solution(mesh):
    placed = (P("col", "row"), P("row", "col"), P("row", "col"), P("row", "col"), P("row", "col"))
    return jax.shard_map(
        on_device,
        mesh=mesh,
        in_specs=placed,
        out_specs=(P("row", "col"), P("row", "col"), P("row", "col")),
        check_vma=False,
    )
```
